256 devices in a mesh: prow: 8 (over z_lo, y), pcol: 32 (over z_hi, x, core).
Axes of the slice: x: 4, y: 4, z: 8 (z_hi: 4, z_lo: 2; z = z_hi * 2 + z_lo), core: 2. Of those that a mesh axis runs over, the one named last changes fastest.
Arguments:
- matrix: bfloat16 [4096, 65536], P('prow', 'pcol'), may hold values from -6 to 6
- pivot_order: int32 [2, 4096], replicated, may hold values from 0 to 4095, as said below
- lower_inverse: float32 [2, 512, 512], replicated, as said below
- upper_inverse: float32 [2, 512, 512], replicated, as said below
Outputs:
- factored: bfloat16 [4096, 65536], P('prow', 'pcol')
The draws below stay inside these ranges and needn't reach their ends.
Inputs may be any that keep to these rules, and one draw needn't show every extreme that they name: pivot_order[k] is a permutation, the product of 512 row swaps, the i-th exchanging row k * 512 + i with a row at or below it. It keeps every row above k * 512 in place, and every row at or below (k + 1) * 512 either stays or takes a row of rows k * 512 to (k + 1) * 512 - 1. lower_inverse[k] is unit lower triangular. upper_inverse[k] is upper triangular with a positive diagonal.
All inputs are finite; a program needn't handle non-finite values.
Results may differ from the reference program's by a relative error of at most 0.0085.
Values may be sent and summed in bfloat16 or wider, within the bound.
A program may use at most 128 MiB of HBM per device.

```python
import math
import jax
import jax.numpy as jnp
from jax import lax

NB = 512
ORDER = 65536
ROWS = 4096
STEPS = 2
N_PROW = 8
N_PCOL = 32


def draw_pivot_order(key, part):
    results = []
    for step_index in range(STEPS):
        subkey = jax.random.fold_in(key, 101 + step_index)
        base_row = step_index * NB
        positions = jnp.arange(NB, dtype=jnp.int32)
        offsets = jax.random.randint(subkey, (NB,), 0, 1 << 30, dtype=jnp.int32)
        targets = base_row + positions + offsets % (ROWS - base_row - positions)

        def swap_rows(index, row_order):
            first_row = base_row + index
            second_row = targets[index]
            first_value = row_order[first_row]
            second_value = row_order[second_row]
            return row_order.at[first_row].set(second_value).at[second_row].set(first_value)
        row_order = lax.fori_loop(0, NB, swap_rows, jnp.arange(ROWS, dtype=jnp.int32))
        results.append(row_order)
    return jnp.stack(results)


def draw_lower_inverse(key, part):
    subkey = jax.random.fold_in(key, 7)
    entries = jax.random.normal(subkey, (STEPS, NB, NB), jnp.float32) * 0.7
    rowsi = jnp.arange(NB)[:, None]
    colsi = jnp.arange(NB)[None, :]
    strict = (rowsi > colsi).astype(jnp.float32)
    unit = (rowsi == colsi).astype(jnp.float32)
    return unit + strict * entries / math.sqrt(NB)


def draw_upper_inverse(key, part):
    first_key = jax.random.fold_in(key, 11)
    second_key = jax.random.fold_in(key, 13)
    entries = jax.random.normal(first_key, (STEPS, NB, NB), jnp.float32) * 0.7
    diagonal = jnp.exp(jax.random.uniform(second_key, (STEPS, 1, NB), jnp.float32, -0.69, 0.69))
    rowsi = jnp.arange(NB)[:, None]
    colsi = jnp.arange(NB)[None, :]
    strict = (rowsi < colsi).astype(jnp.float32)
    unit = (rowsi == colsi).astype(jnp.float32)
    return (unit * diagonal + strict * entries / math.sqrt(NB)) / math.sqrt(NB)


def level_of(own_key, dims, shards, low, high):
    factor_of = 1.0
    for dim, parts in shards:
        steps = jax.random.uniform(jax.random.fold_in(jax.random.fold_in(own_key, 6), dim), (parts,), jnp.float32, low / len(shards), high / len(shards))
        factor_of = factor_of * jnp.repeat(jnp.exp(steps), dims[dim] // parts).reshape((-1,) + (1,) * (len(dims) - 1 - dim))
    return factor_of


def normal_values(rng, extent, scale, most, pieces=(), held_as=jnp.bfloat16):
    level = level_of(rng, extent, pieces, -0.22, 0.18) if pieces else 1.0
    values = jax.random.normal(rng, extent, jnp.float32) * scale * level
    return jnp.minimum(jnp.maximum(values, -most), most).astype(held_as)


def setup_inputs(seed: int = 0) -> dict:
    keys = jax.random.split(jax.random.key(seed), 5)
    return {
        "matrix": normal_values(keys[0], (ROWS, ORDER), 1.0, 6.0, ((0, 8), (1, 32))),
        "pivot_order": draw_pivot_order(jax.random.fold_in(keys[4], 71), 0),
        "lower_inverse": draw_lower_inverse(jax.random.fold_in(keys[4], 71), 0),
        "upper_inverse": draw_upper_inverse(jax.random.fold_in(keys[4], 71), 0),
    }


def to_logical(stored):
    shaped = stored.reshape(N_PROW, ROWS // (N_PROW * NB), NB, N_PCOL, ORDER // (N_PCOL * NB), NB)
    return shaped.transpose(1, 0, 2, 4, 3, 5).reshape(ROWS, ORDER)


def from_logical(logical):
    shaped = logical.reshape(ROWS // (N_PROW * NB), N_PROW, NB, ORDER // (N_PCOL * NB), N_PCOL, NB)
    return shaped.transpose(1, 0, 2, 4, 3, 5).reshape(ROWS, ORDER)


def reference(matrix, pivot_order, lower_inverse, upper_inverse):
    current = to_logical(matrix)
    for step_index in range(STEPS):
        top_begin = step_index * NB
        top_end = top_begin + NB
        current = jnp.take(current, pivot_order[step_index], axis=0)
        top_rows = current[top_begin:top_end, top_end:].astype(jnp.float32)
        solved = jnp.dot(lower_inverse[step_index], top_rows, precision=lax.Precision.HIGHEST).astype(jnp.bfloat16)
        panel_cols = current[top_end:, top_begin:top_end].astype(jnp.float32)
        factor = jnp.dot(panel_cols, upper_inverse[step_index], precision=lax.Precision.HIGHEST).astype(jnp.bfloat16)
        product = jnp.dot(factor, solved, preferred_element_type=jnp.float32)
        trailing = (current[top_end:, top_end:].astype(jnp.float32) - product).astype(jnp.bfloat16)
        current = current.at[top_begin:top_end, top_end:].set(solved)
        current = current.at[top_end:, top_begin:top_end].set(factor)
        current = current.at[top_end:, top_end:].set(trailing)
    return from_logical(current)
```

```python
import jax
import jax.numpy as jnp
from jax import lax
from jax.experimental import pallas as pl
from jax.experimental.pallas import tpu as pltpu
from jax.sharding import PartitionSpec as P

NB = 512
W = 256
BF, F32, I32 = jnp.bfloat16, jnp.float32, jnp.int32
MESH = pl.DeviceIdType.MESH
NEAR = ((1, 0), (3, 0), (2, 0), (0, 1))
FAR = ((1, 1), (3, 1), (2, 1))
PEERS = NEAR + FAR


def mm(a, b):
    return jnp.dot(a, b, preferred_element_type=F32)


def parts(x):
    high = x.astype(BF)
    return high, (x - high.astype(F32)).astype(BF)


def kernel(
    mat, piv, low, upp, out,
    a, raw, cur, fin, res, l0, l1, src, l0p, sel, got, top, lowv, lowh, lowl, uppv, tab, order, t32, u0, u1,
    sem_a, sem_w, sem_o, p1s, p1r, rss, rsr, ags, agr, lps, a1s, ar, a2s, bs, br, cs, cr, ds, dr, p2s, p2r,
):
    p, c = lax.axis_index("prow"), lax.axis_index("pcol")
    zl, y = p // 4, p % 4
    zh, e = c // 8, c % 8
    x, co = e // 2, e % 2
    ls = (l0, l1)

    def peer(dy, dz):
        return (zl + dz) % 2 * 4 + (y + dy) % 4

    def at_x(dx, core):
        return (x + dx) % 4 * 2 + core

    def remote(s, d, ss, rs, to):
        return pltpu.make_async_remote_copy(
            src_ref=s, dst_ref=d, send_sem=ss, recv_sem=rs, device_id=to, device_id_type=MESH
        )

    load = [
        pltpu.make_async_copy(mat.at[:, W * j : W * j + W], a.at[j], sem_a.at[j]) for j in range(8)
    ]
    for cp in load:
        cp.start()
    load_u = pltpu.make_async_copy(upp.at[c % 2], uppv, sem_w.at[0])
    load_u.start()
    load_l = pltpu.make_async_copy(low, lowv, sem_w.at[1])
    load_l.start()

    barrier = pltpu.get_barrier_semaphore()
    for d in PEERS:
        pl.semaphore_signal(barrier, inc=1, device_id=(peer(*d), c), device_id_type=MESH)
    for d in range(1, 8):
        pl.semaphore_signal(barrier, inc=1, device_id=(p, zh * 8 + (e + d) % 8), device_id_type=MESH)
    for d in range(1, 4):
        pl.semaphore_signal(barrier, inc=1, device_id=(p, (zh + d) % 4 * 8 + e), device_id_type=MESH)

    for k in range(2):
        for i in range(32):
            tab[k, i : i + 1, :] = piv[k : k + 1, 128 * i : 128 * i + 128]
    lanes = lax.broadcasted_iota(I32, (NB, 128), 1)
    rows = lax.broadcasted_iota(I32, (NB, 1), 0)

    def looked_up(k, index):
        t = tab[k]
        table = jnp.concatenate([t // 64, t % 64], axis=1).astype(F32).astype(BF)
        hot = jnp.where(lax.broadcasted_iota(I32, (NB, 32), 1) == index // 128, 1.0, 0.0).astype(BF)
        both = mm(hot, table)
        value = both[:, :128] * 64.0 + both[:, 128:]
        return jnp.sum(jnp.where(lanes == index % 128, value, 0.0), axis=1, keepdims=True).astype(I32)

    def hot_rows(index, base, n):
        return jnp.where(lax.broadcasted_iota(I32, (NB, n), 1) + base == index, 1.0, 0.0).astype(BF)

    order[0] = jnp.broadcast_to(looked_up(0, rows), (NB, 128))
    for cp in load:
        cp.wait()
    load_u.wait()
    load_l.wait()
    pl.semaphore_wait(barrier, 17)

    def send_raw(d):
        j = peer(*d)
        return remote(a.at[j], raw.at[p], p1s.at[j], p1r.at[p], (j, c))

    def scatter(k, piece):
        to = zh * 8 + piece
        return remote(src.at[piece], ls[k].at[piece, p], a1s.at[k, piece], ar.at[k], (p, to))

    def share_up(d):
        j = peer(*d)
        return remote(sel.at[j], got.at[p], rss.at[j], rsr.at[p], (j, c))

    def share_top(d):
        j = peer(*d)
        return remote(top.at[p], top.at[p], ags.at[j], agr.at[p], (j, c))

    whole = remote(src, l0p, lps.at[0], lps.at[1], (p, zh * 8 + (e + 1) % 8))

    def panel_factor(first, second):
        uh, ul = parts(uppv[...])
        acc = mm(first, uh[:W]) + mm(second, uh[W:]) + (mm(first, ul[:W]) + mm(second, ul[W:]))
        src[...] = acc.astype(BF).reshape(8, 64, NB)

    @pl.when(c == 0)
    def _():
        panel_factor(a[0], a[1])
        l0[0, p] = src[0]
        for piece in range(1, 8):
            scatter(0, piece).start()
        whole.start()

    @pl.when(c == 1)
    def _():
        hot = hot_rows(order[0, :, 0:1], p * NB, NB)
        for j in range(2):
            sel[:, :, W * j : W * j + W] = mm(hot, a[j]).astype(BF).reshape(8, 64, W)
        got[p] = sel[p]
        for d in PEERS:
            share_up(d).start()

    @pl.when(c >= 2)
    def _():
        for d in NEAR:
            send_raw(d).start()

    def copies(k):
        def up(d):
            to = (zh + d) % 4 * 8 + e
            return remote(ls[k].at[e, p], ls[k].at[e, p], a2s.at[k, d], ar.at[k], (p, to))

        def across(d):
            j = peer(*d)
            return remote(ls[k].at[e, p], ls[k].at[e, p], bs.at[k, j], br.at[k, p], (j, c))

        def over_x(h, d):
            part = ls[k].at[e, pl.ds(4 * h, 4)]
            return remote(part, part, cs.at[k, h, d], cr.at[k, h, x], (p, zh * 8 + at_x(d, co)))

        def over_core(h, d):
            s = at_x(d, co)
            part = ls[k].at[s, pl.ds(4 * h, 4)]
            return remote(part, part, ds.at[k, h, d], dr.at[k, h, s // 2], (p, zh * 8 + at_x(0, 1 - co)))

        def got_x(h, d):
            s = at_x(d, co)
            part = ls[k].at[s, pl.ds(4 * h, 4)]
            return remote(part, part, cs.at[k, h, d], cr.at[k, h, s // 2], (p, zh * 8 + s))

        def got_core(h, d):
            s = at_x(d, 1 - co)
            part = ls[k].at[s, pl.ds(4 * h, 4)]
            return remote(part, part, ds.at[k, h, d], dr.at[k, h, s // 2], (p, zh * 8 + at_x(0, 1 - co)))

        def got_p(d):
            j = peer(*d)
            part = ls[k].at[e, j]
            return remote(part, part, bs.at[k, j], br.at[k, j], (j, c))

        return up, across, over_x, over_core, got_x, got_core, got_p

    kit = (copies(0), copies(1))

    def pass_piece(k):
        up, across = kit[k][:2]

        @pl.when(c != k)
        def _():
            part = ls[k].at[e, p]
            remote(part, part, a1s.at[k, 0], ar.at[k], (p, zh * 8 + (e + 1) % 8)).wait_recv()

        @pl.when(zh == 0)
        def _():
            for d in range(1, 4):
                up(d).start()

        for d in PEERS:
            across(d).start()

    def pass_block(k):
        _, _, over_x, over_core, _, _, got_p = kit[k]
        for d in PEERS:
            got_p(d).wait_recv()
        for h in range(2):
            for d in (1, 3, 2):
                over_x(h, d).start()
            over_core(h, 0).start()

    def take_half(k, h):
        _, _, _, over_core, got_x, got_core, _ = kit[k]
        for d in (1, 3, 2):
            got_x(h, d).wait_recv()
            over_core(h, d).start()
        for d in range(4):
            got_core(h, d).wait_recv()

    pass_piece(0)

    lowh[...] = lowv[...].astype(BF)
    lowl[...] = (lowv[...] - lowh[...].astype(F32)).astype(BF)

    @pl.when(c == 1)
    def _():
        for d in PEERS:
            j = peer(*d)
            remote(sel.at[j], got.at[j], rss.at[j], rsr.at[j], (j, c)).wait_recv()
        total = got[0].astype(F32)
        for j in range(1, 8):
            total = total + got[j].astype(F32)
        top[p] = total.astype(BF)
        for d in PEERS:
            share_top(d).start()
        for d in PEERS:
            j = peer(*d)
            remote(top.at[j], top.at[j], ags.at[j], agr.at[j], (j, c)).wait_recv()
        remote(src, l0p, lps.at[0], lps.at[1], (p, zh * 8 + (e + 7) % 8)).wait_recv()
        tops = top[...].reshape(NB, NB)
        solved = (mm(lowh[0], tops) + mm(lowl[0], tops)).astype(BF)
        less = mm(l0p[...].reshape(NB, NB), solved)
        first = (a[0].astype(F32) - less[:, :W]).astype(BF)
        second = (a[1].astype(F32) - less[:, W:]).astype(BF)
        panel_factor(first, second)
        l1[1, p] = src[1]
        for piece in (0, 2, 3, 4, 5, 6, 7):
            scatter(1, piece).start()

    @pl.when(c < 2)
    def _():
        for d in NEAR:
            send_raw(d).start()

    for d in FAR:
        send_raw(d).start()

    raw[p] = a[p]
    both = jnp.zeros((NB, 128), I32)
    for q in range(1, 8):
        both = jnp.where(lanes == q, looked_up(0, looked_up(1, rows + NB * q)), both)
    order[1] = both

    pass_block(0)
    pass_piece(1)

    for d in PEERS:
        j = peer(*d)
        remote(a.at[j], raw.at[j], p1s.at[j], p1r.at[j], (j, c)).wait_recv()

    def picked(index, ref):
        t32[...] = jnp.zeros((NB, W), F32)

        def add(q, _):
            t32[...] += mm(hot_rows(index, q * NB, NB), ref[q])
            return 0

        lax.fori_loop(0, 8, add, 0)
        return t32[...].astype(BF)

    def solved_by(k, t):
        return (mm(lowh[k], t) + mm(lowl[k], t)).astype(BF)

    own0 = jnp.where(c == 0, 1, 0) * jnp.where(p < 2, 1, 0)
    own1 = jnp.where(c == 1, 1, 0) * jnp.where(p < 2, 1, 0)
    cols = pl.ds(pl.multiple_of(p % 2 * W, W), W)

    t0 = picked(order[0, :, 0:1], raw)
    u0[...] = solved_by(0, t0)

    @pl.when(own0 == 1)
    def _():
        fin[0] = t0

    @pl.when(own0 == 0)
    def _():
        fin[0] = u0[...]

    def send_done(q):
        return remote(fin.at[q], res.at[p], p2s.at[q], p2r.at[p], (q, c))

    def finish(q):
        @pl.when(p == q)
        def _():
            res[q] = fin[q]

        @pl.when(p != q)
        def _():
            send_done(q).start()

    finish(0)
    pass_block(1)
    for h in range(2):
        take_half(0, h)

        def update(q, _):
            @pl.when(own0 == 0)
            def _():
                less = mm(l0[:, q].reshape(NB, NB), u0[...])
                cur[q] = (raw[q].astype(F32) - less).astype(BF)

            @pl.when(own0 == 1)
            def _():
                cur[q] = l0[:, q, :, cols].reshape(NB, W)

            return 0

        lax.fori_loop(4 * h, 4 * h + 4, update, 0)

    t1 = picked(order[1, :, 1:2], cur)
    u1[...] = solved_by(1, t1)

    @pl.when(own0 + own1 == 1)
    def _():
        fin[1] = t1

    @pl.when(own0 + own1 == 0)
    def _():
        fin[1] = u1[...]

    finish(1)
    for h in range(2):
        take_half(1, h)

        def update_again(q, _):
            @pl.when(own0 + own1 == 0)
            def _():
                less = mm(l1[:, q].reshape(NB, NB), u1[...])
                cur[q] = (cur[q].astype(F32) - less).astype(BF)

            @pl.when(own1 == 1)
            def _():
                cur[q] = l1[:, q, :, cols].reshape(NB, W)

            return 0

        lax.fori_loop(4 * h, 4 * h + 4, update_again, 0)
        for q in range(max(4 * h, 2), 4 * h + 4):
            index = order[1, :, q : q + 1]
            moved = mm(hot_rows(index, 0, NB), cur[0]) + mm(hot_rows(index, NB, NB), cur[1])
            fin[q] = jnp.where(index < 2 * NB, moved, cur[q].astype(F32)).astype(BF)
            finish(q)

    def store(j):
        return pltpu.make_async_copy(res.at[j], out.at[:, pl.ds(pl.multiple_of(j * W, W), W)], sem_o.at[j])

    store(p).start()
    for d in PEERS:
        j = peer(*d)
        remote(fin.at[j], res.at[j], p2s.at[j], p2r.at[j], (j, c)).wait_recv()
        store(j).start()

    for d in PEERS:
        send_raw(d).wait_send()
        send_done(peer(*d)).wait_send()
    for k in range(2):
        up, across, over_x, over_core, _, _, _ = kit[k]

        @pl.when(c == k)
        def _():
            for piece in range(8):
                if piece != k:
                    scatter(k, piece).wait_send()

        @pl.when(zh == 0)
        def _():
            for d in range(1, 4):
                up(d).wait_send()

        for d in PEERS:
            across(d).wait_send()
        for h in range(2):
            for d in (1, 3, 2):
                over_x(h, d).wait_send()
            for d in range(4):
                over_core(h, d).wait_send()

    @pl.when(c == 0)
    def _():
        whole.wait_send()

    @pl.when(c == 1)
    def _():
        for d in PEERS:
            share_up(d).wait_send()
            share_top(d).wait_send()

    store(p).wait()
    for d in PEERS:
        store(peer(*d)).wait()


def on_device(matrix, pivot_order, lower_inverse, upper_inverse):
    any_space = pl.BlockSpec(memory_space=pl.ANY)
    dma = pltpu.SemaphoreType.DMA
    shares = pltpu.VMEM((8, NB, W), BF)
    pieces = pltpu.VMEM((8, 64, NB), BF)
    return pl.pallas_call(
        kernel,
        out_shape=jax.ShapeDtypeStruct(matrix.shape, matrix.dtype),
        in_specs=[any_space, pl.BlockSpec(memory_space=pltpu.VMEM), any_space, any_space],
        out_specs=any_space,
        scratch_shapes=[
            shares, shares, shares, shares, shares,
            pltpu.VMEM((8, 8, 64, NB), BF), pltpu.VMEM((8, 8, 64, NB), BF),
            pieces, pieces, pieces, pieces, pieces,
            pltpu.VMEM((2, NB, NB), F32), pltpu.VMEM((2, NB, NB), BF), pltpu.VMEM((2, NB, NB), BF),
            pltpu.VMEM((NB, NB), F32), pltpu.VMEM((2, 32, 128), I32), pltpu.VMEM((2, NB, 128), I32),
            pltpu.VMEM((NB, W), F32), pltpu.VMEM((NB, W), BF), pltpu.VMEM((NB, W), BF),
            dma((8,)), dma((2,)), dma((8,)),
            dma((8,)), dma((8,)), dma((8,)), dma((8,)), dma((8,)), dma((8,)), dma((2,)),
            dma((2, 8)), dma((2,)), dma((2, 4)), dma((2, 8)), dma((2, 8)),
            dma((2, 2, 4)), dma((2, 2, 4)), dma((2, 2, 4)), dma((2, 2, 4)), dma((8,)), dma((8,)),
        ],
        compiler_params=pltpu.CompilerParams(
            collective_id=0, has_side_effects=True, vmem_limit_bytes=60 << 20
        ),
    )(matrix, pivot_order, lower_inverse, upper_inverse)


def solution(mesh):
    return jax.shard_map(
        on_device,
        mesh=mesh,
        in_specs=(P("prow", "pcol"), P(), P(), P()),
        out_specs=P("prow", "pcol"),
        check_vma=False,
    )
```

```python
import jax
import jax.numpy as jnp
from jax import lax
from jax.experimental import pallas as pl
from jax.experimental.pallas import tpu as pltpu
from jax.sharding import PartitionSpec as P

NB = 512
W = 256
BF, F32, I32 = jnp.bfloat16, jnp.float32, jnp.int32
MESH = pl.DeviceIdType.MESH
WAVES = (((1, 0), (3, 0), (2, 0), (0, 1)), ((1, 1), (3, 1), (2, 1)))
PEERS = WAVES[0] + WAVES[1]
AROUND = (1, 3)


def mm(a, b):
    return jnp.dot(a, b, preferred_element_type=F32)


def parts(x):
    high = x.astype(BF)
    return high, (x - high.astype(F32)).astype(BF)


def kernel(
    mat, piv, low, upp, out,
    a, raw, cur, fin, l0, l1, src, l0p, sel, got, top, lowv, lowh, lowl, uppv, tab, order, t32, u0, u1,
    sem_a, sem_w, p1s, p1r, rss, rsr, ags, agr, lps, a1s, ar, a2s, bs, br, cs, cr, ds, dr, p2s, p2r,
):
    p, c = lax.axis_index("prow"), lax.axis_index("pcol")
    zl, y = p // 4, p % 4
    zh, e = c // 8, c % 8
    x, co = e // 2, e % 2
    ls = (l0, l1)

    def peer(dy, dz):
        return (zl + dz) % 2 * 4 + (y + dy) % 4

    def at_x(dx, core):
        return (x + dx) % 4 * 2 + core

    def remote(s, d, ss, rs, to):
        return pltpu.make_async_remote_copy(
            src_ref=s, dst_ref=d, send_sem=ss, recv_sem=rs, device_id=to, device_id_type=MESH
        )

    load = [
        pltpu.make_async_copy(mat.at[:, W * j : W * j + W], a.at[j], sem_a.at[j]) for j in range(8)
    ]
    for cp in load:
        cp.start()
    load_u = pltpu.make_async_copy(upp.at[c % 2], uppv, sem_w.at[0])
    load_u.start()
    load_l = pltpu.make_async_copy(low, lowv, sem_w.at[1])
    load_l.start()

    barrier = pltpu.get_barrier_semaphore()
    for d in PEERS:
        pl.semaphore_signal(barrier, inc=1, device_id=(peer(*d), c), device_id_type=MESH)
    for d in range(1, 8):
        pl.semaphore_signal(barrier, inc=1, device_id=(p, zh * 8 + (e + d) % 8), device_id_type=MESH)
    for d in range(1, 4):
        pl.semaphore_signal(barrier, inc=1, device_id=(p, (zh + d) % 4 * 8 + e), device_id_type=MESH)

    for k in range(2):
        for i in range(32):
            tab[k, i : i + 1, :] = piv[k : k + 1, 128 * i : 128 * i + 128]
    lanes = lax.broadcasted_iota(I32, (NB, 128), 1)
    rows = lax.broadcasted_iota(I32, (NB, 1), 0)

    def looked_up(k, index):
        t = tab[k]
        table = jnp.concatenate([t // 64, t % 64], axis=1).astype(F32).astype(BF)
        hot = jnp.where(lax.broadcasted_iota(I32, (NB, 32), 1) == index // 128, 1.0, 0.0).astype(BF)
        both = mm(hot, table)
        value = both[:, :128] * 64.0 + both[:, 128:]
        return jnp.sum(jnp.where(lanes == index % 128, value, 0.0), axis=1, keepdims=True).astype(I32)

    def hot_rows(index, base, n):
        return jnp.where(lax.broadcasted_iota(I32, (NB, n), 1) + base == index, 1.0, 0.0).astype(BF)

    order[0] = jnp.broadcast_to(looked_up(0, rows), (NB, 128))
    for cp in load:
        cp.wait()
    load_u.wait()
    load_l.wait()
    pl.semaphore_wait(barrier, 17)

    def send_raw(d):
        j = peer(*d)
        return remote(a.at[j], raw.at[p], p1s.at[j], p1r.at[p], (j, c))

    def scatter(k, piece):
        to = zh * 8 + piece
        return remote(src.at[piece], ls[k].at[piece, p], a1s.at[k, piece], ar.at[k], (p, to))

    def share_up(d):
        j = peer(*d)
        return remote(sel.at[j], got.at[p], rss.at[j], rsr.at[p], (j, c))

    def share_top(d):
        j = peer(*d)
        return remote(top.at[p], top.at[p], ags.at[j], agr.at[p], (j, c))

    whole = remote(src, l0p, lps.at[0], lps.at[1], (p, zh * 8 + (e + 1) % 8))

    def panel_factor(first, second):
        uh, ul = parts(uppv[...])
        acc = mm(first, uh[:W]) + mm(second, uh[W:]) + (mm(first, ul[:W]) + mm(second, ul[W:]))
        src[...] = acc.astype(BF).reshape(8, 64, NB)

    @pl.when(c == 0)
    def _():
        panel_factor(a[0], a[1])
        l0[0, p] = src[0]
        for piece in range(1, 8):
            scatter(0, piece).start()
        whole.start()

    @pl.when(c == 1)
    def _():
        hot = hot_rows(order[0, :, 0:1], p * NB, NB)
        for j in range(2):
            sel[:, :, W * j : W * j + W] = mm(hot, a[j]).astype(BF).reshape(8, 64, W)
        got[p] = sel[p]
        for d in PEERS:
            share_up(d).start()

    @pl.when(c >= 2)
    def _():
        for d in WAVES[0]:
            send_raw(d).start()

    def pair(s):
        if s == 0:
            return 0
        high, low_bit = p // 4, p // 2 % 2
        other = (1 - high if s > 1 else high) * 2 + (low_bit if s == 2 else 1 - low_bit)
        return 2 * (other + p // 2 * (1 - (other + 3) // 4))

    def copies(k):
        def up(d):
            to = (zh + d) % 4 * 8 + e
            return remote(ls[k].at[e, p], ls[k].at[e, p], a2s.at[k, d], ar.at[k], (p, to))

        def across(d):
            j = peer(*d)
            return remote(ls[k].at[e, p], ls[k].at[e, p], bs.at[k, j], br.at[k, p], (j, c))

        def block(d, core, s):
            return ls[k].at[at_x(d, core), pl.ds(pair(s), 2)]

        def row_of(d, s, i):
            return ls[k].at[at_x(d, co), pair(s) + i]

        def over_x(s, i):
            part = block(0, co, s)
            return remote(part, part, cs.at[k, s, i], cr.at[k, s, i], (p, zh * 8 + at_x(AROUND[i], co)))

        def onward(s, i):
            part = row_of(AROUND[1 - i], s, i)
            return remote(part, part, cs.at[k, s, 2 + i], cr.at[k, s, 2 + i], (p, zh * 8 + at_x(AROUND[i], co)))

        def over_core(s, d):
            part = block(d, co, s)
            return remote(part, part, ds.at[k, s, d], dr.at[k, s, d], (p, zh * 8 + at_x(0, 1 - co)))

        def got_x(s, i):
            part = block(AROUND[1 - i], co, s)
            return remote(part, part, cs.at[k, s, i], cr.at[k, s, i], (p, zh * 8 + at_x(AROUND[i], co)))

        def got_onward(s, i):
            part = row_of(2, s, i)
            return remote(part, part, cs.at[k, s, 2 + i], cr.at[k, s, 2 + i], (p, zh * 8 + at_x(AROUND[i], co)))

        def got_core(s, d):
            part = block(d, 1 - co, s)
            return remote(part, part, ds.at[k, s, d], dr.at[k, s, d], (p, zh * 8 + at_x(0, 1 - co)))

        return up, across, over_x, onward, over_core, got_x, got_onward, got_core

    kit = (copies(0), copies(1))

    def pass_piece(k):
        up, across = kit[k][:2]

        @pl.when(c != k)
        def _():
            part = ls[k].at[e, p]
            remote(part, part, a1s.at[k, 0], ar.at[k], (p, zh * 8 + (e + 1) % 8)).wait_recv()

        @pl.when(zh == 0)
        def _():
            for d in range(1, 4):
                up(d).start()

        for d in PEERS:
            across(d).start()

    def step(k, s):
        _, _, over_x, _, over_core, _, _, _ = kit[k]
        for i in range(2):
            q = pair(s) + i

            @pl.when(q != p)
            def _():
                part = ls[k].at[e, q]
                remote(part, part, bs.at[k, q], br.at[k, q], (q, c)).wait_recv()

        for i in range(2):
            over_x(s, i).start()
        over_core(s, 0).start()

    def forward(k, s):
        _, _, _, onward, over_core, got_x, _, _ = kit[k]
        for i in range(2):
            got_x(s, i).wait_recv()
            onward(s, i).start()
            over_core(s, AROUND[1 - i]).start()

    def collect(k, s):
        _, _, _, _, over_core, _, got_onward, got_core = kit[k]
        for i in range(2):
            got_onward(s, i).wait_recv()
        over_core(s, 2).start()
        for d in range(4):
            got_core(s, d).wait_recv()

    pass_piece(0)

    lowh[...] = lowv[...].astype(BF)
    lowl[...] = (lowv[...] - lowh[...].astype(F32)).astype(BF)

    @pl.when(c == 1)
    def _():
        for d in PEERS:
            j = peer(*d)
            remote(sel.at[j], got.at[j], rss.at[j], rsr.at[j], (j, c)).wait_recv()
        total = got[0].astype(F32)
        for j in range(1, 8):
            total = total + got[j].astype(F32)
        top[p] = total.astype(BF)
        for d in PEERS:
            share_top(d).start()
        for d in PEERS:
            j = peer(*d)
            remote(top.at[j], top.at[j], ags.at[j], agr.at[j], (j, c)).wait_recv()
        remote(src, l0p, lps.at[0], lps.at[1], (p, zh * 8 + (e + 7) % 8)).wait_recv()
        tops = top[...].reshape(NB, NB)
        solved = (mm(lowh[0], tops) + mm(lowl[0], tops)).astype(BF)
        less = mm(l0p[...].reshape(NB, NB), solved)
        first = (a[0].astype(F32) - less[:, :W]).astype(BF)
        second = (a[1].astype(F32) - less[:, W:]).astype(BF)
        panel_factor(first, second)
        l1[1, p] = src[1]
        for piece in (0, 2, 3, 4, 5, 6, 7):
            scatter(1, piece).start()

    @pl.when(c < 2)
    def _():
        for d in WAVES[0]:
            send_raw(d).start()

    for d in WAVES[1]:
        send_raw(d).start()

    raw[p] = a[p]
    both = jnp.zeros((NB, 128), I32)
    for q in range(1, 8):
        both = jnp.where(lanes == q, looked_up(0, looked_up(1, rows + NB * q)), both)
    order[1] = both

    step(0, 0)
    step(0, 1)
    forward(0, 0)
    step(0, 2)
    forward(0, 1)
    step(0, 3)
    pass_piece(1)
    forward(0, 2)
    forward(0, 3)

    for d in PEERS:
        j = peer(*d)
        remote(a.at[j], raw.at[j], p1s.at[j], p1r.at[j], (j, c)).wait_recv()

    def picked(index, ref):
        t32[...] = jnp.zeros((NB, W), F32)

        def add(q, _):
            t32[...] += mm(hot_rows(index, q * NB, NB), ref[q])
            return 0

        lax.fori_loop(0, 8, add, 0)
        return t32[...].astype(BF)

    def solved_by(k, t):
        return (mm(lowh[k], t) + mm(lowl[k], t)).astype(BF)

    own0 = jnp.where(c == 0, 1, 0) * jnp.where(p < 2, 1, 0)
    own1 = jnp.where(c == 1, 1, 0) * jnp.where(p < 2, 1, 0)
    cols = pl.ds(pl.multiple_of(p % 2 * W, W), W)

    t0 = picked(order[0, :, 0:1], raw)
    u0[...] = solved_by(0, t0)

    @pl.when(own0 == 1)
    def _():
        fin[0] = t0

    @pl.when(own0 == 0)
    def _():
        fin[0] = u0[...]

    mine = pl.ds(pl.multiple_of(p * W, W), W)

    def send_done(q):
        return remote(fin.at[q], out.at[:, mine], p2s.at[q], p2r.at[p], (q, c))

    step(1, 0)
    step(1, 1)

    def update(s):
        collect(0, s)
        for i in range(2):
            q = pair(s) + i

            @pl.when(own0 == 0)
            def _():
                less = mm(l0[:, q].reshape(NB, NB), u0[...])
                cur[q] = (raw[q].astype(F32) - less).astype(BF)

            @pl.when(own0 == 1)
            def _():
                cur[q] = l0[:, q, :, cols].reshape(NB, W)

    update(0)
    update(1)
    forward(1, 0)
    step(1, 2)
    update(2)
    update(3)
    forward(1, 1)
    step(1, 3)
    t1 = picked(order[1, :, 1:2], cur)
    u1[...] = solved_by(1, t1)

    @pl.when(own0 + own1 == 1)
    def _():
        fin[1] = t1

    @pl.when(own0 + own1 == 0)
    def _():
        fin[1] = u1[...]

    def update_again(s):
        collect(1, s)
        for i in range(2):
            q = pair(s) + (i + p) % 2

            @pl.when(own0 + own1 == 0)
            def _():
                less = mm(l1[:, q].reshape(NB, NB), u1[...])
                cur[q] = (cur[q].astype(F32) - less).astype(BF)

            @pl.when(own1 == 1)
            def _():
                cur[q] = l1[:, q, :, cols].reshape(NB, W)

            if s:
                index = jnp.sum(
                    jnp.where(lanes == q, order[1].astype(F32), 0.0), axis=1, keepdims=True
                ).astype(I32)
                moved = mm(hot_rows(index, 0, NB), cur[0]) + mm(hot_rows(index, NB, NB), cur[1])
                fin[q] = jnp.where(index < 2 * NB, moved, cur[q].astype(F32)).astype(BF)

    forward(1, 2)
    update_again(0)
    forward(1, 3)
    for s in range(1, 4):
        update_again(s)

    out[:, mine] = fin[p]
    for d in PEERS:
        send_done(peer(*d)).start()

    for d in PEERS:
        j = peer(*d)
        part = out.at[:, pl.ds(pl.multiple_of(j * W, W), W)]
        remote(fin.at[j], part, p2s.at[j], p2r.at[j], (j, c)).wait_recv()

    for d in PEERS:
        send_raw(d).wait_send()
        send_done(peer(*d)).wait_send()
    for k in range(2):
        up, across, over_x, onward, over_core, _, _, _ = kit[k]

        @pl.when(c == k)
        def _():
            for piece in range(8):
                if piece != k:
                    scatter(k, piece).wait_send()

        @pl.when(zh == 0)
        def _():
            for d in range(1, 4):
                up(d).wait_send()

        for d in PEERS:
            across(d).wait_send()
        for s in range(4):
            for i in range(2):
                over_x(s, i).wait_send()
                onward(s, i).wait_send()
            for d in range(4):
                over_core(s, d).wait_send()

    @pl.when(c == 0)
    def _():
        whole.wait_send()

    @pl.when(c == 1)
    def _():
        for d in PEERS:
            share_up(d).wait_send()
            share_top(d).wait_send()


def on_device(matrix, pivot_order, lower_inverse, upper_inverse):
    any_space = pl.BlockSpec(memory_space=pl.ANY)
    dma = pltpu.SemaphoreType.DMA
    shares = pltpu.VMEM((8, NB, W), BF)
    pieces = pltpu.VMEM((8, 64, NB), BF)
    return pl.pallas_call(
        kernel,
        out_shape=pltpu.VMEM(matrix.shape, matrix.dtype),
        in_specs=[any_space, pl.BlockSpec(memory_space=pltpu.VMEM), any_space, any_space],
        out_specs=pl.BlockSpec(memory_space=pltpu.VMEM),
        scratch_shapes=[
            shares, shares, shares, shares,
            pltpu.VMEM((8, 8, 64, NB), BF), pltpu.VMEM((8, 8, 64, NB), BF),
            pieces, pieces, pieces, pieces, pieces,
            pltpu.VMEM((2, NB, NB), F32), pltpu.VMEM((2, NB, NB), BF), pltpu.VMEM((2, NB, NB), BF),
            pltpu.VMEM((NB, NB), F32), pltpu.VMEM((2, 32, 128), I32), pltpu.VMEM((2, NB, 128), I32),
            pltpu.VMEM((NB, W), F32), pltpu.VMEM((NB, W), BF), pltpu.VMEM((NB, W), BF),
            dma((8,)), dma((2,)),
            dma((8,)), dma((8,)), dma((8,)), dma((8,)), dma((8,)), dma((8,)), dma((2,)),
            dma((2, 8)), dma((2,)), dma((2, 4)), dma((2, 8)), dma((2, 8)),
            dma((2, 4, 4)), dma((2, 4, 4)), dma((2, 4, 4)), dma((2, 4, 4)), dma((8,)), dma((8,)),
        ],
        compiler_params=pltpu.CompilerParams(
            collective_id=0, has_side_effects=True, vmem_limit_bytes=60 << 20
        ),
    )(matrix, pivot_order, lower_inverse, upper_inverse)


def solution(mesh):
    return jax.shard_map(
        on_device,
        mesh=mesh,
        in_specs=(P("prow", "pcol"), P(), P(), P()),
        out_specs=P("prow", "pcol"),
        check_vma=False,
    )
```

```python
import jax
import jax.numpy as jnp
from jax import lax
from jax.experimental import pallas as pl
from jax.experimental.pallas import tpu as pltpu
from jax.sharding import PartitionSpec as P

NB = 512
W = 256
BF, F32, I32 = jnp.bfloat16, jnp.float32, jnp.int32
MESH = pl.DeviceIdType.MESH
WAVES = (((1, 0), (3, 0), (2, 0), (0, 1)), ((1, 1), (3, 1), (2, 1)))
PEERS = WAVES[0] + WAVES[1]
AROUND = (1, 3)


def mm(a, b):
    return jnp.dot(a, b, preferred_element_type=F32)


def parts(x):
    high = x.astype(BF)
    return high, (x - high.astype(F32)).astype(BF)


def kernel(
    mat, piv, low, upp, out,
    a, raw, cur, fin, l0, l1, src, l0p, sel, got, top, lowv, lowh, lowl, uppv, tab, order, t32, u0, u1,
    sem_a, sem_w, p1s, p1r, rss, rsr, ags, agr, lps, a1s, ar, a2s, bs, br, cs, cr, ds, dr, p2s, p2r,
):
    p, c = lax.axis_index("prow"), lax.axis_index("pcol")
    zl, y = p // 4, p % 4
    zh, e = c // 8, c % 8
    x, co = e // 2, e % 2
    ls = (l0, l1)

    def peer(dy, dz):
        return (zl + dz) % 2 * 4 + (y + dy) % 4

    def at_x(dx, core):
        return (x + dx) % 4 * 2 + core

    def remote(s, d, ss, rs, to):
        return pltpu.make_async_remote_copy(
            src_ref=s, dst_ref=d, send_sem=ss, recv_sem=rs, device_id=to, device_id_type=MESH
        )

    load = [
        pltpu.make_async_copy(mat.at[:, W * j : W * j + W], a.at[j], sem_a.at[j]) for j in range(8)
    ]
    for cp in load:
        cp.start()
    load_u = pltpu.make_async_copy(upp.at[c % 2], uppv, sem_w.at[0])
    load_u.start()
    load_l = pltpu.make_async_copy(low, lowv, sem_w.at[1])
    load_l.start()

    barrier = pltpu.get_barrier_semaphore()
    for d in PEERS:
        pl.semaphore_signal(barrier, inc=1, device_id=(peer(*d), c), device_id_type=MESH)
    for d in range(1, 8):
        pl.semaphore_signal(barrier, inc=1, device_id=(p, zh * 8 + (e + d) % 8), device_id_type=MESH)
    for d in range(1, 4):
        pl.semaphore_signal(barrier, inc=1, device_id=(p, (zh + d) % 4 * 8 + e), device_id_type=MESH)

    for k in range(2):
        for i in range(32):
            tab[k, i : i + 1, :] = piv[k : k + 1, 128 * i : 128 * i + 128]
    lanes = lax.broadcasted_iota(I32, (NB, 128), 1)
    rows = lax.broadcasted_iota(I32, (NB, 1), 0)

    def looked_up(k, index):
        t = tab[k]
        table = jnp.concatenate([t // 64, t % 64], axis=1).astype(F32).astype(BF)
        hot = jnp.where(lax.broadcasted_iota(I32, (NB, 32), 1) == index // 128, 1.0, 0.0).astype(BF)
        both = mm(hot, table)
        value = both[:, :128] * 64.0 + both[:, 128:]
        return jnp.sum(jnp.where(lanes == index % 128, value, 0.0), axis=1, keepdims=True).astype(I32)

    def hot_rows(index, base, n):
        return jnp.where(lax.broadcasted_iota(I32, (NB, n), 1) + base == index, 1.0, 0.0).astype(BF)

    order[0] = jnp.broadcast_to(looked_up(0, rows), (NB, 128))
    for cp in load:
        cp.wait()
    load_u.wait()
    load_l.wait()
    pl.semaphore_wait(barrier, 17)

    def send_raw(d):
        j = peer(*d)
        return remote(a.at[j], raw.at[p], p1s.at[j], p1r.at[p], (j, c))

    def scatter(k, piece):
        to = zh * 8 + piece
        return remote(src.at[piece], ls[k].at[piece, p], a1s.at[k, piece], ar.at[k], (p, to))

    def share_up(d):
        j = peer(*d)
        return remote(sel.at[j], got.at[p], rss.at[j], rsr.at[p], (j, c))

    def share_top(d):
        j = peer(*d)
        return remote(top.at[p], top.at[p], ags.at[j], agr.at[p], (j, c))

    whole = remote(src, l0p, lps.at[0], lps.at[1], (p, zh * 8 + (e + 1) % 8))

    def panel_factor(first, second):
        uh, ul = parts(uppv[...])
        acc = mm(first, uh[:W]) + mm(second, uh[W:]) + (mm(first, ul[:W]) + mm(second, ul[W:]))
        src[...] = acc.astype(BF).reshape(8, 64, NB)

    @pl.when(c == 0)
    def _():
        panel_factor(a[0], a[1])
        l0[0, p] = src[0]
        for piece in range(1, 8):
            scatter(0, piece).start()
        whole.start()

    @pl.when(c == 1)
    def _():
        hot = hot_rows(order[0, :, 0:1], p * NB, NB)
        for j in range(2):
            sel[:, :, W * j : W * j + W] = mm(hot, a[j]).astype(BF).reshape(8, 64, W)
        got[p] = sel[p]
        for d in PEERS:
            share_up(d).start()

    @pl.when(c >= 2)
    def _():
        for d in WAVES[0]:
            send_raw(d).start()

    def pair(s):
        if s == 0:
            return 0
        high, low_bit = p // 4, p // 2 % 2
        other = (1 - high if s > 1 else high) * 2 + (low_bit if s == 2 else 1 - low_bit)
        return 2 * (other + p // 2 * (1 - (other + 3) // 4))

    def copies(k):
        def up(d):
            to = (zh + d) % 4 * 8 + e
            return remote(ls[k].at[e, p], ls[k].at[e, p], a2s.at[k, d], ar.at[k], (p, to))

        def across(d):
            j = peer(*d)
            return remote(ls[k].at[e, p], ls[k].at[e, p], bs.at[k, j], br.at[k, p], (j, c))

        def block(d, core, s):
            return ls[k].at[at_x(d, core), pl.ds(pair(s), 2)]

        def row_of(d, s, i):
            return ls[k].at[at_x(d, co), pair(s) + i]

        def over_x(s, i):
            part = block(0, co, s)
            return remote(part, part, cs.at[k, s, i], cr.at[k, s, i], (p, zh * 8 + at_x(AROUND[i], co)))

        def onward(s, i):
            part = row_of(AROUND[1 - i], s, i)
            return remote(part, part, cs.at[k, s, 2 + i], cr.at[k, s, 2 + i], (p, zh * 8 + at_x(AROUND[i], co)))

        def over_core(s, d):
            part = block(d, co, s)
            return remote(part, part, ds.at[k, s, d], dr.at[k, s, d], (p, zh * 8 + at_x(0, 1 - co)))

        def got_x(s, i):
            part = block(AROUND[1 - i], co, s)
            return remote(part, part, cs.at[k, s, i], cr.at[k, s, i], (p, zh * 8 + at_x(AROUND[i], co)))

        def got_onward(s, i):
            part = row_of(2, s, i)
            return remote(part, part, cs.at[k, s, 2 + i], cr.at[k, s, 2 + i], (p, zh * 8 + at_x(AROUND[i], co)))

        def got_core(s, d):
            part = block(d, 1 - co, s)
            return remote(part, part, ds.at[k, s, d], dr.at[k, s, d], (p, zh * 8 + at_x(0, 1 - co)))

        return up, across, over_x, onward, over_core, got_x, got_onward, got_core

    kit = (copies(0), copies(1))

    def pass_piece(k):
        up, across = kit[k][:2]

        @pl.when(c != k)
        def _():
            part = ls[k].at[e, p]
            remote(part, part, a1s.at[k, 0], ar.at[k], (p, zh * 8 + (e + 1) % 8)).wait_recv()

        @pl.when(zh == 0)
        def _():
            for d in range(1, 4):
                up(d).start()

        for d in PEERS:
            across(d).start()

    def step(k, s):
        _, _, over_x, _, over_core, _, _, _ = kit[k]
        for i in range(2):
            q = pair(s) + i

            @pl.when(q != p)
            def _():
                part = ls[k].at[e, q]
                remote(part, part, bs.at[k, q], br.at[k, q], (q, c)).wait_recv()

        for i in range(2):
            over_x(s, i).start()
        over_core(s, 0).start()

    def forward(k, s):
        _, _, _, onward, over_core, got_x, _, _ = kit[k]
        for i in range(2):
            got_x(s, i).wait_recv()
            onward(s, i).start()
            over_core(s, AROUND[1 - i]).start()

    def collect(k, s):
        _, _, _, _, over_core, _, got_onward, got_core = kit[k]
        for i in range(2):
            got_onward(s, i).wait_recv()
        over_core(s, 2).start()
        for d in range(4):
            got_core(s, d).wait_recv()

    pass_piece(0)

    lowh[...] = lowv[...].astype(BF)
    lowl[...] = (lowv[...] - lowh[...].astype(F32)).astype(BF)

    @pl.when(c == 1)
    def _():
        for d in PEERS:
            j = peer(*d)
            remote(sel.at[j], got.at[j], rss.at[j], rsr.at[j], (j, c)).wait_recv()
        total = got[0].astype(F32)
        for j in range(1, 8):
            total = total + got[j].astype(F32)
        top[p] = total.astype(BF)
        for d in PEERS:
            share_top(d).start()
        for d in PEERS:
            j = peer(*d)
            remote(top.at[j], top.at[j], ags.at[j], agr.at[j], (j, c)).wait_recv()
        remote(src, l0p, lps.at[0], lps.at[1], (p, zh * 8 + (e + 7) % 8)).wait_recv()
        tops = top[...].reshape(NB, NB)
        solved = (mm(lowh[0], tops) + mm(lowl[0], tops)).astype(BF)
        less = mm(l0p[...].reshape(NB, NB), solved)
        first = (a[0].astype(F32) - less[:, :W]).astype(BF)
        second = (a[1].astype(F32) - less[:, W:]).astype(BF)
        panel_factor(first, second)
        l1[1, p] = src[1]
        for piece in (0, 2, 3, 4, 5, 6, 7):
            scatter(1, piece).start()

    @pl.when(c < 2)
    def _():
        for d in WAVES[0]:
            send_raw(d).start()

    for d in WAVES[1]:
        send_raw(d).start()

    raw[p] = a[p]
    both = jnp.zeros((NB, 128), I32)
    for q in range(1, 8):
        both = jnp.where(lanes == q, looked_up(0, looked_up(1, rows + NB * q)), both)
    order[1] = both

    step(0, 0)
    step(0, 1)
    forward(0, 0)
    step(0, 2)
    forward(0, 1)
    step(0, 3)
    pass_piece(1)
    forward(0, 2)
    forward(0, 3)

    for d in PEERS:
        j = peer(*d)
        remote(a.at[j], raw.at[j], p1s.at[j], p1r.at[j], (j, c)).wait_recv()

    def picked(index, ref):
        t32[...] = jnp.zeros((NB, W), F32)

        def add(q, _):
            t32[...] += mm(hot_rows(index, q * NB, NB), ref[q])
            return 0

        lax.fori_loop(0, 8, add, 0)
        return t32[...].astype(BF)

    def solved_by(k, t):
        return (mm(lowh[k], t) + mm(lowl[k], t)).astype(BF)

    own0 = jnp.where(c == 0, 1, 0) * jnp.where(p < 2, 1, 0)
    own1 = jnp.where(c == 1, 1, 0) * jnp.where(p < 2, 1, 0)
    cols = pl.ds(pl.multiple_of(p % 2 * W, W), W)

    t0 = picked(order[0, :, 0:1], raw)
    u0[...] = solved_by(0, t0)

    @pl.when(own0 == 1)
    def _():
        fin[0] = t0

    @pl.when(own0 == 0)
    def _():
        fin[0] = u0[...]

    mine = pl.ds(pl.multiple_of(p * W, W), W)

    def send_done(q):
        return remote(fin.at[q], out.at[:, mine], p2s.at[q], p2r.at[p], (q, c))

    step(1, 0)
    step(1, 1)

    def update(s):
        collect(0, s)
        for i in range(2):
            q = pair(s) + i

            @pl.when(own0 == 0)
            def _():
                less = mm(l0[:, q].reshape(NB, NB), u0[...])
                cur[q] = (raw[q].astype(F32) - less).astype(BF)

            @pl.when(own0 == 1)
            def _():
                cur[q] = l0[:, q, :, cols].reshape(NB, W)

    update(0)
    update(1)
    forward(1, 0)
    step(1, 2)
    update(2)
    update(3)
    forward(1, 1)
    step(1, 3)
    t1 = picked(order[1, :, 1:2], cur)
    u1[...] = solved_by(1, t1)

    @pl.when(own0 + own1 == 1)
    def _():
        fin[1] = t1

    @pl.when(own0 + own1 == 0)
    def _():
        fin[1] = u1[...]

    def update_again(s):
        collect(1, s)
        for i in range(2):
            q = pair(s) + (i + p) % 2

            @pl.when(own0 + own1 == 0)
            def _():
                less = mm(l1[:, q].reshape(NB, NB), u1[...])
                cur[q] = (cur[q].astype(F32) - less).astype(BF)

            @pl.when(own1 == 1)
            def _():
                cur[q] = l1[:, q, :, cols].reshape(NB, W)

            if s:
                index = jnp.sum(
                    jnp.where(lanes == q, order[1].astype(F32), 0.0), axis=1, keepdims=True
                ).astype(I32)
                moved = mm(hot_rows(index, 0, NB), cur[0]) + mm(hot_rows(index, NB, NB), cur[1])
                fin[q] = jnp.where(index < 2 * NB, moved, cur[q].astype(F32)).astype(BF)

    forward(1, 2)
    update_again(0)
    forward(1, 3)
    def send_if(wanted):
        for d in PEERS:
            q = peer(*d)

            @pl.when(wanted(q // 2))
            def _():
                send_done(q).start()

    send_if(lambda two: two == 0)
    update_again(1)
    update_again(2)
    send_if(lambda two: two == pair(1) // 2)
    update_again(3)
    out[:, mine] = fin[p]
    send_if(lambda two: (two != 0) & (two != pair(1) // 2))

    for d in PEERS:
        j = peer(*d)
        part = out.at[:, pl.ds(pl.multiple_of(j * W, W), W)]
        remote(fin.at[j], part, p2s.at[j], p2r.at[j], (j, c)).wait_recv()

    for d in PEERS:
        send_raw(d).wait_send()
        send_done(peer(*d)).wait_send()
    for k in range(2):
        up, across, over_x, onward, over_core, _, _, _ = kit[k]

        @pl.when(c == k)
        def _():
            for piece in range(8):
                if piece != k:
                    scatter(k, piece).wait_send()

        @pl.when(zh == 0)
        def _():
            for d in range(1, 4):
                up(d).wait_send()

        for d in PEERS:
            across(d).wait_send()
        for s in range(4):
            for i in range(2):
                over_x(s, i).wait_send()
                onward(s, i).wait_send()
            for d in range(4):
                over_core(s, d).wait_send()

    @pl.when(c == 0)
    def _():
        whole.wait_send()

    @pl.when(c == 1)
    def _():
        for d in PEERS:
            share_up(d).wait_send()
            share_top(d).wait_send()


def on_device(matrix, pivot_order, lower_inverse, upper_inverse):
    any_space = pl.BlockSpec(memory_space=pl.ANY)
    dma = pltpu.SemaphoreType.DMA
    shares = pltpu.VMEM((8, NB, W), BF)
    pieces = pltpu.VMEM((8, 64, NB), BF)
    return pl.pallas_call(
        kernel,
        out_shape=pltpu.VMEM(matrix.shape, matrix.dtype),
        in_specs=[any_space, pl.BlockSpec(memory_space=pltpu.VMEM), any_space, any_space],
        out_specs=pl.BlockSpec(memory_space=pltpu.VMEM),
        scratch_shapes=[
            shares, shares, shares, shares,
            pltpu.VMEM((8, 8, 64, NB), BF), pltpu.VMEM((8, 8, 64, NB), BF),
            pieces, pieces, pieces, pieces, pieces,
            pltpu.VMEM((2, NB, NB), F32), pltpu.VMEM((2, NB, NB), BF), pltpu.VMEM((2, NB, NB), BF),
            pltpu.VMEM((NB, NB), F32), pltpu.VMEM((2, 32, 128), I32), pltpu.VMEM((2, NB, 128), I32),
            pltpu.VMEM((NB, W), F32), pltpu.VMEM((NB, W), BF), pltpu.VMEM((NB, W), BF),
            dma((8,)), dma((2,)),
            dma((8,)), dma((8,)), dma((8,)), dma((8,)), dma((8,)), dma((8,)), dma((2,)),
            dma((2, 8)), dma((2,)), dma((2, 4)), dma((2, 8)), dma((2, 8)),
            dma((2, 4, 4)), dma((2, 4, 4)), dma((2, 4, 4)), dma((2, 4, 4)), dma((8,)), dma((8,)),
        ],
        compiler_params=pltpu.CompilerParams(
            collective_id=0, has_side_effects=True, vmem_limit_bytes=60 << 20
        ),
    )(matrix, pivot_order, lower_inverse, upper_inverse)


def solution(mesh):
    return jax.shard_map(
        on_device,
        mesh=mesh,
        in_specs=(P("prow", "pcol"), P(), P(), P()),
        out_specs=P("prow", "pcol"),
        check_vma=False,
    )
```
